32 devices in a mesh: seq: 8 (over z, x), chan: 4 (over y, core).
Axes of the slice: x: 2, y: 2, z: 4, core: 2. Of those that a mesh axis runs over, the one named last changes fastest.
Arguments:
- values: bfloat16 [2048, 4096], P('seq', 'chan'), may hold values from -6 to 6
- gates: bfloat16 [2048, 4096], P('seq', 'chan'), may hold values from -6 to 6
- filters: float32 [2048, 4096], P('seq', 'chan'), may hold values from -4 to 4
- skip: float32 [4096], P('chan'), may hold values from -1 to 1
- w_out: bfloat16 [4096, 4096], P(None, 'chan'), may hold values from -0.09375 to 0.09375
Outputs:
- output: bfloat16 [2048, 4096], P('seq', 'chan')
The draws below stay inside these ranges and needn't reach their ends.
All inputs are finite; a program needn't handle non-finite values.
Results may differ from the reference program's by a relative error of at most 0.0056.
Values may be sent and summed in bfloat16 or wider, within the bound.
A program may use at most 128 MiB of HBM per device.

```python
import jax
import jax.numpy as jnp
from jax import lax

D = 4096
TOKENS = 2048


def draw_filters(key, part):
    rate_key, noise_key = jax.random.split(key)
    lags = lax.iota(jnp.float32, TOKENS)[:, None]
    log_rate = jax.random.uniform(rate_key, (1, D), jnp.float32, jnp.log(0.01 / TOKENS), jnp.log(1.0 / 30.0))
    noise = jax.random.truncated_normal(noise_key, -4.0, 4.0, (TOKENS, D), jnp.float32)
    rate = jnp.exp(log_rate)
    scale = jnp.sqrt(1.0 - jnp.exp(-2.0 * rate))
    return noise * scale * jnp.exp(-rate * lags)


def level_of(stream_key, dims, cuts, least, high):
    def one(position, blocks):
        heights = jax.random.uniform(jax.random.fold_in(jax.random.fold_in(stream_key, 6), position), (blocks,), jnp.float32, least / len(cuts), high / len(cuts))
        return jnp.repeat(jnp.exp(heights), dims[position] // blocks).reshape((-1,) + (1,) * (len(dims) - position - 1))

    gain = one(*cuts[0])
    for cut in cuts[1:]:
        gain = gain * one(*cut)
    return gain


def scatter_about(stream_key, extent, deviation, reach, cuts=(), held_as=jnp.bfloat16):
    entries = deviation * jax.random.normal(stream_key, extent, jnp.float32)
    if cuts:
        entries = entries * level_of(stream_key, extent, cuts, -0.22, 0.18)
    return jnp.clip(entries, -reach, reach).astype(held_as)


def setup_inputs(seed: int = 0) -> dict:
    keys = jax.random.split(jax.random.key(seed), 6)
    return {
        "values": scatter_about(keys[0], (TOKENS, D), 1.0, 6.0, ((0, 8), (1, 4))),
        "gates": scatter_about(keys[1], (TOKENS, D), 1.0, 6.0, ((0, 8), (1, 4))),
        "filters": draw_filters(jax.random.fold_in(keys[5], 71), 0),
        "skip": jnp.clip(jax.random.uniform(keys[3], (D,), jnp.float32, -1.0, 1.0) * level_of(keys[3], (D,), ((0, 4),), -0.4, 0.0), -1.0, 1.0),
        "w_out": scatter_about(keys[4], (D, D), D ** -0.5, 0.09375, ((1, 4),)),
    }


def reference(values, gates, filters, skip, w_out):
    length = values.shape[0]
    channels = values.shape[1]
    block_width = min(512, channels)
    block_count = channels // block_width
    signal = values.astype(jnp.float32).T.reshape(block_count, block_width, length)
    kernel = filters.astype(jnp.float32).T.reshape(block_count, block_width, length)

    def convolve(operands):
        signal_block, kernel_block = operands
        spectrum = jnp.fft.rfft(signal_block, n=2 * length, axis=1) * jnp.fft.rfft(kernel_block, n=2 * length, axis=1)
        return jnp.fft.irfft(spectrum, n=2 * length, axis=1)[:, :length]

    causal = lax.map(convolve, (signal, kernel)).reshape(channels, length).T.astype(jnp.bfloat16)
    mixed = (gates.astype(jnp.float32) * (causal.astype(jnp.float32) + skip[None, :] * values.astype(jnp.float32))).astype(jnp.bfloat16)
    return jnp.dot(mixed, w_out, preferred_element_type=jnp.float32).astype(jnp.bfloat16)
```

```python
import functools
import math

import jax
import jax.numpy as jnp
import numpy as np
from jax import lax
from jax.experimental import pallas as pl
from jax.experimental.pallas import tpu as pltpu
from jax.sharding import PartitionSpec as P

LANES = 128
STRIP = 16
MESH = pl.DeviceIdType.MESH


def product(form, left, right):
    return jnp.einsum(
        form, left, right, precision=lax.Precision.HIGHEST, preferred_element_type=jnp.float32
    )


def phase(first_count, second_count, modulus):
    left = lax.iota(jnp.int32, first_count)[:, None]
    right = lax.iota(jnp.int32, second_count)[None, :]
    angle = (left * right % modulus).astype(jnp.float32) * (2.0 * math.pi / modulus)
    return (jnp.cos(angle), jnp.sin(angle))


def spectral_conv(chan_values, chan_filter):
    nchan = chan_values.shape[0]
    length = chan_values.shape[1]
    summed = 2 * length
    columns = 128
    row_count = summed // columns
    half_rows = row_count // 2
    cos_rows, sin_rows = phase(row_count, half_rows, row_count)
    cos_twist, sin_twist = phase(row_count, columns, summed)
    cos_cols, sin_cols = phase(columns, columns, columns)
    cos_back, sin_back = phase(half_rows, row_count, row_count)

    def forward(signal):
        grid = signal.astype(jnp.float32).reshape(nchan, half_rows, columns)
        real_a = product("kn,cna->cka", cos_rows, grid)
        imag_a = -product("kn,cna->cka", sin_rows, grid)
        real_b = real_a * cos_twist + imag_a * sin_twist
        imag_b = imag_a * cos_twist - real_a * sin_twist
        real_c = product("cka,am->ckm", real_b, cos_cols) + product("cka,am->ckm", imag_b, sin_cols)
        imag_c = product("cka,am->ckm", imag_b, cos_cols) - product("cka,am->ckm", real_b, sin_cols)
        return (real_c, imag_c)

    real_v, imag_v = forward(chan_values)
    real_h, imag_h = forward(chan_filter)
    real_p = real_v * real_h - imag_v * imag_h
    imag_p = real_v * imag_h + imag_v * real_h
    real_d = product("ckm,ma->cka", real_p, cos_cols) - product("ckm,ma->cka", imag_p, sin_cols)
    imag_d = product("ckm,ma->cka", imag_p, cos_cols) + product("ckm,ma->cka", real_p, sin_cols)
    real_e = real_d * cos_twist - imag_d * sin_twist
    imag_e = imag_d * cos_twist + real_d * sin_twist
    result = product("nk,cka->cna", cos_back, real_e) - product("nk,cka->cna", sin_back, imag_e)
    return (result * (1.0 / summed)).reshape(nchan, length).astype(jnp.bfloat16)


def per_device_generic(values, gates, filters, skip, w_out):
    value_trans = values.T
    filter_trans = filters.T
    chan_values = lax.all_to_all(value_trans, "seq", split_axis=0, concat_axis=1, tiled=True)
    chan_filter = lax.all_to_all(filter_trans, "seq", split_axis=0, concat_axis=1, tiled=True)
    convolved = spectral_conv(chan_values, chan_filter)
    causal_trans = lax.all_to_all(convolved, "seq", split_axis=1, concat_axis=0, tiled=True)
    causal = causal_trans.T
    mixed = (
        gates.astype(jnp.float32)
        * (causal.astype(jnp.float32) + skip[None, :] * values.astype(jnp.float32))
    ).astype(jnp.bfloat16)
    projected = jnp.dot(
        lax.all_gather(mixed, "chan", axis=1, tiled=True), w_out, preferred_element_type=jnp.float32
    )
    return projected.astype(jnp.bfloat16)


def split(x):
    high = x.astype(jnp.bfloat16)
    return high, (x - high.astype(jnp.float32)).astype(jnp.bfloat16)


def tables(blocks, block):
    index = np.arange(block)
    angle = 2.0 * np.pi * (np.outer(index, index) % block) / block
    cos, sin = np.cos(angle), np.sin(angle)
    whole = np.block([[cos, sin], [-sin, cos]]).astype(np.float32)
    high = whole.astype(jnp.bfloat16)
    low = (whole - high.astype(np.float32)).astype(jnp.bfloat16)
    turn = 2.0 * np.pi * np.outer(index, np.arange(blocks) + 0.5) / (2 * blocks * block)
    twiddle = np.zeros((block, LANES), np.float32)
    twiddle[:, :blocks] = np.cos(turn)
    twiddle[:, blocks : 2 * blocks] = np.sin(turn)
    return np.stack([high, low]), twiddle


def weighted(terms):
    total = None
    for weight, term in terms:
        part = term if weight == 1.0 else term * np.float32(weight)
        total = part if total is None else total + part
    return total


def kernel(
    blocks, chans,
    values, gates, filters, skip, dft, twiddle, w_hbm,
    out,
    h_send, got_v, got_h, z, y, d, y_send, causal, mixed, w, acc,
    w_sem, v_out, v_in, h_out, h_in, c_out, c_in, a_out, a_in, b_out, b_in, f_out, f_in,
):
    me = lax.axis_index("seq")
    mine = lax.axis_index("chan")
    block = values.shape[0]
    half = blocks // 2

    def columns(position):
        return pl.ds(pl.multiple_of(position * LANES, LANES), LANES)

    def ahead(step):
        return lax.rem(me + step, blocks)

    def behind(step):
        return lax.rem(me + blocks - step, blocks)

    w_copy = pltpu.make_async_copy(w_hbm, w, w_sem)
    w_copy.start()

    sibling = mine + 1 - 2 * lax.rem(mine, 2)
    across = lax.rem(mine + 2, chans)
    barrier = pltpu.get_barrier_semaphore()
    for step in range(1, blocks):
        pl.semaphore_signal(barrier, inc=1, device_id={"seq": ahead(step)}, device_id_type=MESH)
    for other in (sibling, across):
        pl.semaphore_signal(barrier, inc=1, device_id={"chan": other}, device_id_type=MESH)
    pl.semaphore_wait(barrier, blocks + 1)

    def exchange(source, target, out_sem, in_sem, step):
        return pltpu.make_async_remote_copy(
            src_ref=source.at[:, columns(ahead(step))],
            dst_ref=target.at[me],
            send_sem=out_sem.at[step],
            recv_sem=in_sem.at[step],
            device_id={"seq": ahead(step)},
            device_id_type=MESH,
        )

    order = sorted(range(1, blocks), key=lambda step: -min(step, blocks - step))
    v_copies = [exchange(values, got_v, v_out, v_in, step) for step in order]
    for copy in v_copies:
        copy.start()
    h_send[...] = filters[...].astype(jnp.bfloat16)
    h_copies = [exchange(h_send, got_h, h_out, h_in, step) for step in order]
    for copy in h_copies:
        copy.start()
    got_v[me] = values[:, columns(me)]
    got_h[me] = h_send[:, columns(me)]
    for copy in v_copies + h_copies:
        copy.wait()

    def spread(strip, _):
        rows = pl.ds(pl.multiple_of(strip * STRIP, STRIP), STRIP)
        for side, got in enumerate((got_v, got_h)):
            lanes = slice(side * LANES, (side + 1) * LANES)
            x = [got[n, rows, :].astype(jnp.float32) for n in range(blocks)]
            for r in range(half):
                phi = math.pi * (2 * r + 1) / (2 * blocks)
                sums = []
                for odd in (0, 1):
                    picks = range(odd, blocks, 2)
                    sums.append(weighted([(math.cos(phi * n), x[n]) for n in picks]))
                    sums.append(weighted([(-math.sin(phi * n), x[n]) for n in picks if n]))
                even_re, even_im, odd_re, odd_im = sums
                for res, re, im in (
                    (r, even_re + odd_re, even_im + odd_im),
                    (blocks - 1 - r, even_re - odd_re, odd_im - even_im),
                ):
                    cos = twiddle[rows, res : res + 1]
                    sin = twiddle[rows, blocks + res : blocks + res + 1]
                    re_high, re_low = split(re * cos + im * sin)
                    im_high, im_low = split(im * cos - re * sin)
                    for place, part in enumerate((re_high, im_high, re_low, im_low)):
                        z[res, pl.ds(place * block + strip * STRIP, STRIP), lanes] = part
        return 0

    lax.fori_loop(0, block // STRIP, spread, 0)

    def times(x):
        return (
            jnp.dot(dft[0], x[: 2 * block], preferred_element_type=jnp.float32)
            + jnp.dot(dft[1], x[: 2 * block], preferred_element_type=jnp.float32)
            + jnp.dot(dft[0], x[2 * block :], preferred_element_type=jnp.float32)
        )

    def middle(pair, _):
        for which in range(2):
            x = times(z[2 * pair + which])
            lanes = slice(which * LANES, (which + 1) * LANES)
            re_v, re_h = x[:block, :LANES], x[:block, LANES:]
            im_v, im_h = x[block:, :LANES], x[block:, LANES:]
            re_high, re_low = split(re_v * re_h - im_v * im_h)
            im_high, im_low = split(-(re_v * im_h + im_v * re_h))
            for place, part in enumerate((re_high, im_high, re_low, im_low)):
                y[place * block : (place + 1) * block, lanes] = part
        d[pair] = times(y[...])
        return 0

    lax.fori_loop(0, half, middle, 0)

    def gather(strip, _):
        rows = pl.ds(pl.multiple_of(strip * STRIP, STRIP), STRIP)
        scale = 1.0 / (blocks * block)
        parts = []
        for r in range(half):
            turned = []
            for res in (r, blocks - 1 - r):
                lanes = slice(res % 2 * LANES, (res % 2 + 1) * LANES)
                re = d[res // 2, rows, lanes]
                im = -d[res // 2, pl.ds(block + strip * STRIP, STRIP), lanes]
                cos = twiddle[rows, res : res + 1]
                sin = twiddle[rows, blocks + res : blocks + res + 1]
                turned.append((re * cos - im * sin, im * cos + re * sin))
            (re_a, im_a), (re_b, im_b) = turned
            parts.append(((re_a + re_b, im_a - im_b), (re_a - re_b, im_a + im_b)))
        for n in range(blocks):
            terms = []
            for r in range(half):
                phi = math.pi * (2 * r + 1) / (2 * blocks)
                re, im = parts[r][n % 2]
                terms.append((scale * math.cos(phi * n), re))
                if n:
                    terms.append((-scale * math.sin(phi * n), im))
            y_send[n, rows, :] = weighted(terms).astype(jnp.bfloat16)
        return 0

    lax.fori_loop(0, block // STRIP, gather, 0)

    c_copies = {
        step: pltpu.make_async_remote_copy(
            src_ref=y_send.at[ahead(step)],
            dst_ref=causal.at[me],
            send_sem=c_out.at[step],
            recv_sem=c_in.at[step],
            device_id={"seq": ahead(step)},
            device_id_type=MESH,
        )
        for step in order
    }
    for step in order:
        c_copies[step].start()
    causal[me] = y_send[me]

    def share(source_chan, source_block, target, out_sem, in_sem, step):
        spot = mixed.at[source_chan, :, columns(source_block)]
        return pltpu.make_async_remote_copy(
            src_ref=spot, dst_ref=spot,
            send_sem=out_sem.at[step], recv_sem=in_sem.at[step],
            device_id={"chan": target}, device_id_type=MESH,
        )

    arrival = [0] + order[::-1]
    a_copies, b_copies, f_copies = [], [], []
    for step in arrival:
        source = behind(step)
        if step:
            c_copies[step].wait_recv()
        cols = columns(source)
        direct = skip[:, cols] * values[:, cols].astype(jnp.float32)
        mixed[mine, :, cols] = (
            gates[:, cols].astype(jnp.float32) * (causal[source].astype(jnp.float32) + direct)
        ).astype(jnp.bfloat16)
        a_copies.append(share(mine, source, across, a_out, a_in, step))
        b_copies.append(share(mine, source, sibling, b_out, b_in, step))
        a_copies[-1].start()
        b_copies[-1].start()

    w_copy.wait()
    depth = values.shape[1]

    def project(which, first, last):
        def tile(n, _):
            cols = pl.ds(pl.multiple_of(n * 256, 256), 256)
            rows = pl.ds(pl.multiple_of(which * depth, depth), depth)
            part = jnp.dot(mixed[which], w[rows, cols], preferred_element_type=jnp.float32)
            if not first:
                part = part + acc[:, cols]
            if last:
                out[:, cols] = part.astype(out.dtype)
            else:
                acc[:, cols] = part
            return 0

        lax.fori_loop(0, out.shape[1] // 256, tile, 0)

    project(mine, True, False)
    for index, step in enumerate(arrival):
        a_copies[index].wait_recv()
        f_copies.append(share(across, behind(step), sibling, f_out, f_in, step))
        f_copies[-1].start()
    for copy in b_copies:
        copy.wait_recv()
    project(sibling, False, False)
    project(across, False, False)
    for copy in f_copies:
        copy.wait_recv()
    project(lax.rem(sibling + 2, chans), False, True)
    for copy in a_copies + b_copies + f_copies + list(c_copies.values()):
        copy.wait_send()


def per_device_fused(blocks, chans, values, gates, filters, skip, w_out):
    block, width = values.shape
    dft, twiddle = tables(blocks, block)
    vmem = pl.BlockSpec(memory_space=pltpu.VMEM)
    sems = pltpu.SemaphoreType.DMA((blocks,))
    half = blocks // 2
    return pl.pallas_call(
        functools.partial(kernel, blocks, chans),
        out_shape=jax.ShapeDtypeStruct((block, w_out.shape[1]), jnp.bfloat16),
        in_specs=[vmem] * 6 + [pl.BlockSpec(memory_space=pl.ANY)],
        out_specs=vmem,
        scratch_shapes=[
            pltpu.VMEM((block, width), jnp.bfloat16),
            pltpu.VMEM((blocks, block, LANES), jnp.bfloat16),
            pltpu.VMEM((blocks, block, LANES), jnp.bfloat16),
            pltpu.VMEM((blocks, 4 * block, 2 * LANES), jnp.bfloat16),
            pltpu.VMEM((4 * block, 2 * LANES), jnp.bfloat16),
            pltpu.VMEM((half, 2 * block, 2 * LANES), jnp.float32),
            pltpu.VMEM((blocks, block, LANES), jnp.bfloat16),
            pltpu.VMEM((blocks, block, LANES), jnp.bfloat16),
            pltpu.VMEM((chans, block, width), jnp.bfloat16),
            pltpu.VMEM(w_out.shape, jnp.bfloat16),
            pltpu.VMEM((block, w_out.shape[1]), jnp.float32),
            pltpu.SemaphoreType.DMA,
        ]
        + [sems] * 12,
        compiler_params=pltpu.CompilerParams(
            collective_id=0, has_side_effects=True, vmem_limit_bytes=56 * 2**20
        ),
    )(values, gates, filters, skip[None, :], jnp.asarray(dft), jnp.asarray(twiddle), w_out)


def per_device(mesh_shape, values, gates, filters, skip, w_out):
    blocks, chans = mesh_shape["seq"], mesh_shape["chan"]
    block, width = values.shape
    fits = (
        width == blocks * LANES and chans == 4 and blocks % 2 == 0 and blocks <= 16
        and block % 256 == 0 and block <= 512 and w_out.shape[1] % 256 == 0
    )
    if fits:
        return per_device_fused(blocks, chans, values, gates, filters, skip, w_out)
    return per_device_generic(values, gates, filters, skip, w_out)


def solution(mesh):
    placed = (P("seq", "chan"), P("seq", "chan"), P("seq", "chan"), P("chan"), P(None, "chan"))
    return jax.shard_map(
        functools.partial(per_device, dict(mesh.shape)),
        mesh=mesh, in_specs=placed, out_specs=P("seq", "chan"), check_vma=False,
    )
```

```python
import functools
import math

import jax
import jax.numpy as jnp
import numpy as np
from jax import lax
from jax.experimental import pallas as pl
from jax.experimental.pallas import tpu as pltpu
from jax.sharding import PartitionSpec as P

LANES = 128
STRIP = 16
IN_PARTS = 2
OUT_PARTS = 4
MESH = pl.DeviceIdType.MESH


def product(form, left, right):
    return jnp.einsum(
        form, left, right, precision=lax.Precision.HIGHEST, preferred_element_type=jnp.float32
    )


def phase(first_count, second_count, modulus):
    left = lax.iota(jnp.int32, first_count)[:, None]
    right = lax.iota(jnp.int32, second_count)[None, :]
    angle = (left * right % modulus).astype(jnp.float32) * (2.0 * math.pi / modulus)
    return (jnp.cos(angle), jnp.sin(angle))


def spectral_conv(chan_values, chan_filter):
    nchan = chan_values.shape[0]
    length = chan_values.shape[1]
    summed = 2 * length
    columns = 128
    row_count = summed // columns
    half_rows = row_count // 2
    cos_rows, sin_rows = phase(row_count, half_rows, row_count)
    cos_twist, sin_twist = phase(row_count, columns, summed)
    cos_cols, sin_cols = phase(columns, columns, columns)
    cos_back, sin_back = phase(half_rows, row_count, row_count)

    def forward(signal):
        grid = signal.astype(jnp.float32).reshape(nchan, half_rows, columns)
        real_a = product("kn,cna->cka", cos_rows, grid)
        imag_a = -product("kn,cna->cka", sin_rows, grid)
        real_b = real_a * cos_twist + imag_a * sin_twist
        imag_b = imag_a * cos_twist - real_a * sin_twist
        real_c = product("cka,am->ckm", real_b, cos_cols) + product("cka,am->ckm", imag_b, sin_cols)
        imag_c = product("cka,am->ckm", imag_b, cos_cols) - product("cka,am->ckm", real_b, sin_cols)
        return (real_c, imag_c)

    real_v, imag_v = forward(chan_values)
    real_h, imag_h = forward(chan_filter)
    real_p = real_v * real_h - imag_v * imag_h
    imag_p = real_v * imag_h + imag_v * real_h
    real_d = product("ckm,ma->cka", real_p, cos_cols) - product("ckm,ma->cka", imag_p, sin_cols)
    imag_d = product("ckm,ma->cka", imag_p, cos_cols) + product("ckm,ma->cka", real_p, sin_cols)
    real_e = real_d * cos_twist - imag_d * sin_twist
    imag_e = imag_d * cos_twist + real_d * sin_twist
    result = product("nk,cka->cna", cos_back, real_e) - product("nk,cka->cna", sin_back, imag_e)
    return (result * (1.0 / summed)).reshape(nchan, length).astype(jnp.bfloat16)


def per_device_generic(values, gates, filters, skip, w_out):
    value_trans = values.T
    filter_trans = filters.T
    chan_values = lax.all_to_all(value_trans, "seq", split_axis=0, concat_axis=1, tiled=True)
    chan_filter = lax.all_to_all(filter_trans, "seq", split_axis=0, concat_axis=1, tiled=True)
    convolved = spectral_conv(chan_values, chan_filter)
    causal_trans = lax.all_to_all(convolved, "seq", split_axis=1, concat_axis=0, tiled=True)
    causal = causal_trans.T
    mixed = (
        gates.astype(jnp.float32)
        * (causal.astype(jnp.float32) + skip[None, :] * values.astype(jnp.float32))
    ).astype(jnp.bfloat16)
    projected = jnp.dot(
        lax.all_gather(mixed, "chan", axis=1, tiled=True), w_out, preferred_element_type=jnp.float32
    )
    return projected.astype(jnp.bfloat16)


def split(x):
    high = x.astype(jnp.bfloat16)
    return high, (x - high.astype(jnp.float32)).astype(jnp.bfloat16)


def tables(blocks, block, parts):
    index = np.arange(block)
    angle = 2.0 * np.pi * (np.outer(index, index) % block) / block
    cos, sin = np.cos(angle), np.sin(angle)
    whole = np.block([[cos, sin], [-sin, cos]]).astype(np.float32)
    high = whole.astype(jnp.bfloat16)
    both = np.stack([high, (whole - high.astype(np.float32)).astype(jnp.bfloat16)])

    def members(count):
        size = block // count
        return [np.concatenate([index[p * size : (p + 1) * size] + block * i for i in (0, 1)]) for p in range(count)]

    forward = np.stack([both[:, :, m] for m in members(IN_PARTS)])
    backward = np.stack([both[:, m, :] for m in members(parts)])
    turn = 2.0 * np.pi * np.outer(index, np.arange(blocks) + 0.5) / (2 * blocks * block)
    twiddle = np.zeros((block, LANES), np.float32)
    twiddle[:, :blocks] = np.cos(turn)
    twiddle[:, blocks : 2 * blocks] = np.sin(turn)
    return forward, backward, twiddle


def weighted(terms):
    total = None
    for weight, term in terms:
        part = term if weight == 1.0 else term * np.float32(weight)
        total = part if total is None else total + part
    return total


def kernel(
    blocks, chans, parts,
    values_hbm, gates_hbm, filters_hbm, skip, forward_hbm, backward_hbm, twiddle, w_hbm,
    out,
    values, gates, filters, h_send, got_v, got_h, forward, backward, z, spec_v, spec_h, y, d, y_send, causal, mixed, w, acc,
    l_sem, v_out, v_in, h_out, h_in, c_out, c_in, a_out, a_in, b_out, b_in, f_out, f_in,
):
    me = lax.axis_index("seq")
    mine = lax.axis_index("chan")
    block = values.shape[0]
    half = blocks // 2
    piece = block // IN_PARTS
    chunk = block // parts

    def columns(position):
        return pl.ds(pl.multiple_of(position * LANES, LANES), LANES)

    def ahead(step):
        return lax.rem(me + step, blocks)

    def behind(step):
        return lax.rem(me + blocks - step, blocks)

    local = [
        pltpu.make_async_copy(source, target, l_sem.at[i])
        for i, (source, target) in enumerate((
            (filters_hbm, filters), (values_hbm, values), (values_hbm.at[:, columns(me)], got_v.at[me]),
            (forward_hbm, forward), (backward_hbm, backward), (gates_hbm, gates), (w_hbm, w),
        ))
    ]
    filters_copy, values_copy, own_copy, forward_copy, backward_copy, gates_copy, w_copy = local
    for copy in local:
        copy.start()

    sibling = mine + 1 - 2 * lax.rem(mine, 2)
    across = lax.rem(mine + 2, chans)
    barrier = pltpu.get_barrier_semaphore()
    for step in range(1, blocks):
        pl.semaphore_signal(barrier, inc=1, device_id={"seq": ahead(step)}, device_id_type=MESH)
    for other in (sibling, across):
        pl.semaphore_signal(barrier, inc=1, device_id={"chan": other}, device_id_type=MESH)
    pl.semaphore_wait(barrier, blocks + 1)

    def exchange(source, target, out_sem, in_sem, part, step):
        rows = pl.ds(part * piece, piece)
        return pltpu.make_async_remote_copy(
            src_ref=source.at[rows, columns(ahead(step))],
            dst_ref=target.at[me, rows],
            send_sem=out_sem.at[part, step],
            recv_sem=in_sem.at[part, step],
            device_id={"seq": ahead(step)},
            device_id_type=MESH,
        )

    order = sorted(range(1, blocks), key=lambda step: -min(step, blocks - step))
    v_copies = [[exchange(values_hbm, got_v, v_out, v_in, part, step) for step in order] for part in range(IN_PARTS)]
    for copies in v_copies:
        for copy in copies:
            copy.start()
    filters_copy.wait()
    h_copies = [[exchange(h_send, got_h, h_out, h_in, part, step) for step in order] for part in range(IN_PARTS)]
    for part in range(IN_PARTS):
        rows = pl.ds(part * piece, piece)
        h_send[rows, :] = filters[rows, :].astype(jnp.bfloat16)
        for copy in h_copies[part]:
            copy.start()
    got_h[me] = h_send[:, columns(me)]
    own_copy.wait()
    forward_copy.wait()

    def spread(got, part):
        def body(strip, _):
            here = pl.multiple_of(strip * STRIP, STRIP)
            rows = pl.ds(part * piece + here, STRIP)
            x = [got[n, rows, :].astype(jnp.float32) for n in range(blocks)]
            for r in range(half):
                phi = math.pi * (2 * r + 1) / (2 * blocks)
                sums = []
                for odd in (0, 1):
                    picks = range(odd, blocks, 2)
                    sums.append(weighted([(math.cos(phi * n), x[n]) for n in picks]))
                    sums.append(weighted([(-math.sin(phi * n), x[n]) for n in picks if n]))
                even_re, even_im, odd_re, odd_im = sums
                for res, re, im in (
                    (r, even_re + odd_re, even_im + odd_im),
                    (blocks - 1 - r, even_re - odd_re, odd_im - even_im),
                ):
                    cos = twiddle[rows, res : res + 1]
                    sin = twiddle[rows, blocks + res : blocks + res + 1]
                    lanes = slice(res % 2 * LANES, (res % 2 + 1) * LANES)
                    re_high, re_low = split(re * cos + im * sin)
                    im_high, im_low = split(im * cos - re * sin)
                    for place, value in enumerate((re_high, im_high, re_low, im_low)):
                        z[res // 2, pl.ds(place * piece + here, STRIP), lanes] = value
            return 0

        lax.fori_loop(0, piece // STRIP, body, 0)

    def times(high, low, x):
        middle = x.shape[0] // 2
        return (
            jnp.dot(high, x[:middle], preferred_element_type=jnp.float32)
            + jnp.dot(low, x[:middle], preferred_element_type=jnp.float32)
            + jnp.dot(high, x[middle:], preferred_element_type=jnp.float32)
        )

    def transform(spectrum, part):
        def body(pair, _):
            x = times(forward[part, 0], forward[part, 1], z[pair])
            spectrum[pair] = spectrum[pair] + x if part else x
            return 0

        lax.fori_loop(0, half, body, 0)

    for got, copies, spectrum in ((got_v, v_copies, spec_v), (got_h, h_copies, spec_h)):
        for part in range(IN_PARTS):
            for copy in copies[part]:
                copy.wait_recv()
            spread(got, part)
            transform(spectrum, part)

    def product(pair, _):
        re_v, re_h = spec_v[pair, :block], spec_h[pair, :block]
        im_v, im_h = spec_v[pair, block:], spec_h[pair, block:]
        re_high, re_low = split(re_v * re_h - im_v * im_h)
        im_high, im_low = split(-(re_v * im_h + im_v * re_h))
        for place, value in enumerate((re_high, im_high, re_low, im_low)):
            y[pair, place * block : (place + 1) * block] = value
        return 0

    lax.fori_loop(0, half, product, 0)
    backward_copy.wait()

    def undo(part):
        def inverse(pair, _):
            d[pair] = times(backward[part, 0], backward[part, 1], y[pair])
            return 0

        lax.fori_loop(0, half, inverse, 0)

        def body(strip, _):
            here = pl.multiple_of(strip * STRIP, STRIP)
            rows = pl.ds(part * chunk + here, STRIP)
            scale = 1.0 / (blocks * block)
            sums = []
            for r in range(half):
                turned = []
                for res in (r, blocks - 1 - r):
                    lanes = slice(res % 2 * LANES, (res % 2 + 1) * LANES)
                    re = d[res // 2, pl.ds(here, STRIP), lanes]
                    im = -d[res // 2, pl.ds(chunk + here, STRIP), lanes]
                    cos = twiddle[rows, res : res + 1]
                    sin = twiddle[rows, blocks + res : blocks + res + 1]
                    turned.append((re * cos - im * sin, im * cos + re * sin))
                (re_a, im_a), (re_b, im_b) = turned
                sums.append(((re_a + re_b, im_a - im_b), (re_a - re_b, im_a + im_b)))
            for n in range(blocks):
                terms = []
                for r in range(half):
                    phi = math.pi * (2 * r + 1) / (2 * blocks)
                    re, im = sums[r][n % 2]
                    terms.append((scale * math.cos(phi * n), re))
                    if n:
                        terms.append((-scale * math.sin(phi * n), im))
                y_send[n, rows, :] = weighted(terms).astype(jnp.bfloat16)
            return 0

        lax.fori_loop(0, chunk // STRIP, body, 0)

    c_copies = []
    for part in range(parts):
        undo(part)
        rows = pl.ds(part * chunk, chunk)
        c_copies.append([
            pltpu.make_async_remote_copy(
                src_ref=y_send.at[ahead(step), rows],
                dst_ref=causal.at[me, rows],
                send_sem=c_out.at[part, step],
                recv_sem=c_in.at[part, step],
                device_id={"seq": ahead(step)},
                device_id_type=MESH,
            )
            for step in order
        ])
        for copy in c_copies[part]:
            copy.start()
        causal[me, rows] = y_send[me, rows]

    def share(source_chan, target, out_sem, in_sem, part):
        spot = mixed.at[source_chan, pl.ds(part * chunk, chunk)]
        return pltpu.make_async_remote_copy(
            src_ref=spot, dst_ref=spot,
            send_sem=out_sem.at[part], recv_sem=in_sem.at[part],
            device_id={"chan": target}, device_id_type=MESH,
        )

    depth = values.shape[1]
    a_copies = [share(mine, across, a_out, a_in, part) for part in range(parts)]
    b_copies = [share(mine, sibling, b_out, b_in, part) for part in range(parts)]
    f_copies = [share(across, sibling, f_out, f_in, part) for part in range(parts)]
    opposite = lax.rem(sibling + 2, chans)

    def blend(part):
        rows = pl.ds(part * chunk, chunk)
        for source in range(blocks):
            cols = slice(source * LANES, (source + 1) * LANES)
            direct = skip[:, cols] * values[rows, cols].astype(jnp.float32)
            mixed[mine, rows, cols] = (
                gates[rows, cols].astype(jnp.float32) * (causal[source, rows].astype(jnp.float32) + direct)
            ).astype(jnp.bfloat16)

    def project(part, pair, last):
        rows = pl.ds(part * chunk, chunk)

        def tile(n, _):
            cols = pl.ds(pl.multiple_of(n * 256, 256), 256)
            total = None
            for which in pair:
                deep = pl.ds(pl.multiple_of(which * depth, depth), depth)
                term = jnp.dot(mixed[which, rows], w[deep, cols], preferred_element_type=jnp.float32)
                total = term if total is None else total + term
            if last:
                out[rows, cols] = (total + acc[rows, cols]).astype(out.dtype)
            else:
                acc[rows, cols] = total
            return 0

        lax.fori_loop(0, out.shape[1] // 256, tile, 0)

    def finish(part):
        f_copies[part].wait_recv()
        project(part, (across, opposite), True)

    values_copy.wait()
    gates_copy.wait()
    w_copy.wait()
    for part in range(parts):
        for copy in c_copies[part]:
            copy.wait_recv()
        blend(part)
        a_copies[part].start()
        b_copies[part].start()
        if part >= 1:
            a_copies[part - 1].wait_recv()
            f_copies[part - 1].start()
        b_copies[part].wait_recv()
        project(part, (mine, sibling), False)
        if part >= 1 and part < parts - 1:
            finish(part - 1)
    a_copies[parts - 1].wait_recv()
    f_copies[parts - 1].start()
    if parts >= 2:
        finish(parts - 2)
    finish(parts - 1)
    for copies in v_copies + h_copies + c_copies + [a_copies, b_copies, f_copies]:
        for copy in copies:
            copy.wait_send()


def per_device_fused(blocks, chans, values, gates, filters, skip, w_out):
    block, width = values.shape
    parts = OUT_PARTS
    forward, backward, twiddle = tables(blocks, block, parts)
    vmem = pl.BlockSpec(memory_space=pltpu.VMEM)
    hbm = pl.BlockSpec(memory_space=pl.ANY)
    half = blocks // 2
    out_width = w_out.shape[1]

    def sems(*shape):
        return pltpu.SemaphoreType.DMA(shape)

    return pl.pallas_call(
        functools.partial(kernel, blocks, chans, parts),
        out_shape=jax.ShapeDtypeStruct((block, out_width), jnp.bfloat16),
        in_specs=[hbm, hbm, hbm, vmem, hbm, hbm, vmem, hbm],
        out_specs=vmem,
        scratch_shapes=[
            pltpu.VMEM((block, width), jnp.bfloat16),
            pltpu.VMEM((block, width), jnp.bfloat16),
            pltpu.VMEM((block, width), jnp.float32),
            pltpu.VMEM((block, width), jnp.bfloat16),
            pltpu.VMEM((blocks, block, LANES), jnp.bfloat16),
            pltpu.VMEM((blocks, block, LANES), jnp.bfloat16),
            pltpu.VMEM(forward.shape, jnp.bfloat16),
            pltpu.VMEM(backward.shape, jnp.bfloat16),
            pltpu.VMEM((half, 4 * block // IN_PARTS, 2 * LANES), jnp.bfloat16),
            pltpu.VMEM((half, 2 * block, 2 * LANES), jnp.float32),
            pltpu.VMEM((half, 2 * block, 2 * LANES), jnp.float32),
            pltpu.VMEM((half, 4 * block, 2 * LANES), jnp.bfloat16),
            pltpu.VMEM((half, 2 * block // parts, 2 * LANES), jnp.float32),
            pltpu.VMEM((blocks, block, LANES), jnp.bfloat16),
            pltpu.VMEM((blocks, block, LANES), jnp.bfloat16),
            pltpu.VMEM((chans, block, width), jnp.bfloat16),
            pltpu.VMEM(w_out.shape, jnp.bfloat16),
            pltpu.VMEM((block, out_width), jnp.float32),
            sems(7),
        ]
        + [sems(IN_PARTS, blocks)] * 4
        + [sems(parts, blocks)] * 2
        + [sems(parts)] * 6,
        compiler_params=pltpu.CompilerParams(
            collective_id=0, has_side_effects=True, vmem_limit_bytes=56 * 2**20
        ),
    )(values, gates, filters, skip[None, :], jnp.asarray(forward), jnp.asarray(backward), jnp.asarray(twiddle), w_out)


def per_device(mesh_shape, values, gates, filters, skip, w_out):
    blocks, chans = mesh_shape["seq"], mesh_shape["chan"]
    block, width = values.shape
    fits = (
        width == blocks * LANES and chans == 4 and blocks % 2 == 0 and blocks <= 16
        and block % 256 == 0 and block <= 512 and w_out.shape[1] % 256 == 0
    )
    if fits:
        return per_device_fused(blocks, chans, values, gates, filters, skip, w_out)
    return per_device_generic(values, gates, filters, skip, w_out)


def solution(mesh):
    placed = (P("seq", "chan"), P("seq", "chan"), P("seq", "chan"), P("chan"), P(None, "chan"))
    return jax.shard_map(
        functools.partial(per_device, dict(mesh.shape)),
        mesh=mesh, in_specs=placed, out_specs=P("seq", "chan"), check_vma=False,
    )
```

```python
import functools
import math

import jax
import jax.numpy as jnp
import numpy as np
from jax import lax
from jax.experimental import pallas as pl
from jax.experimental.pallas import tpu as pltpu
from jax.sharding import PartitionSpec as P

LANES = 128
STRIP = 16
IN_PARTS = 2
OUT_PARTS = 4
LAG = 2
MESH = pl.DeviceIdType.MESH


def product(form, left, right):
    return jnp.einsum(
        form, left, right, precision=lax.Precision.HIGHEST, preferred_element_type=jnp.float32
    )


def phase(first_count, second_count, modulus):
    left = lax.iota(jnp.int32, first_count)[:, None]
    right = lax.iota(jnp.int32, second_count)[None, :]
    angle = (left * right % modulus).astype(jnp.float32) * (2.0 * math.pi / modulus)
    return (jnp.cos(angle), jnp.sin(angle))


def spectral_conv(chan_values, chan_filter):
    nchan = chan_values.shape[0]
    length = chan_values.shape[1]
    summed = 2 * length
    columns = 128
    row_count = summed // columns
    half_rows = row_count // 2
    cos_rows, sin_rows = phase(row_count, half_rows, row_count)
    cos_twist, sin_twist = phase(row_count, columns, summed)
    cos_cols, sin_cols = phase(columns, columns, columns)
    cos_back, sin_back = phase(half_rows, row_count, row_count)

    def forward(signal):
        grid = signal.astype(jnp.float32).reshape(nchan, half_rows, columns)
        real_a = product("kn,cna->cka", cos_rows, grid)
        imag_a = -product("kn,cna->cka", sin_rows, grid)
        real_b = real_a * cos_twist + imag_a * sin_twist
        imag_b = imag_a * cos_twist - real_a * sin_twist
        real_c = product("cka,am->ckm", real_b, cos_cols) + product("cka,am->ckm", imag_b, sin_cols)
        imag_c = product("cka,am->ckm", imag_b, cos_cols) - product("cka,am->ckm", real_b, sin_cols)
        return (real_c, imag_c)

    real_v, imag_v = forward(chan_values)
    real_h, imag_h = forward(chan_filter)
    real_p = real_v * real_h - imag_v * imag_h
    imag_p = real_v * imag_h + imag_v * real_h
    real_d = product("ckm,ma->cka", real_p, cos_cols) - product("ckm,ma->cka", imag_p, sin_cols)
    imag_d = product("ckm,ma->cka", imag_p, cos_cols) + product("ckm,ma->cka", real_p, sin_cols)
    real_e = real_d * cos_twist - imag_d * sin_twist
    imag_e = imag_d * cos_twist + real_d * sin_twist
    result = product("nk,cka->cna", cos_back, real_e) - product("nk,cka->cna", sin_back, imag_e)
    return (result * (1.0 / summed)).reshape(nchan, length).astype(jnp.bfloat16)


def per_device_generic(values, gates, filters, skip, w_out):
    value_trans = values.T
    filter_trans = filters.T
    chan_values = lax.all_to_all(value_trans, "seq", split_axis=0, concat_axis=1, tiled=True)
    chan_filter = lax.all_to_all(filter_trans, "seq", split_axis=0, concat_axis=1, tiled=True)
    convolved = spectral_conv(chan_values, chan_filter)
    causal_trans = lax.all_to_all(convolved, "seq", split_axis=1, concat_axis=0, tiled=True)
    causal = causal_trans.T
    mixed = (
        gates.astype(jnp.float32)
        * (causal.astype(jnp.float32) + skip[None, :] * values.astype(jnp.float32))
    ).astype(jnp.bfloat16)
    projected = jnp.dot(
        lax.all_gather(mixed, "chan", axis=1, tiled=True), w_out, preferred_element_type=jnp.float32
    )
    return projected.astype(jnp.bfloat16)


def split(x):
    high = x.astype(jnp.bfloat16)
    return high, (x - high.astype(jnp.float32)).astype(jnp.bfloat16)


def tables(blocks, block, parts):
    index = np.arange(block)
    angle = 2.0 * np.pi * (np.outer(index, index) % block) / block
    cos, sin = np.cos(angle), np.sin(angle)
    whole = np.block([[cos, sin], [-sin, cos]]).astype(np.float32)
    high = whole.astype(jnp.bfloat16)
    both = np.stack([high, (whole - high.astype(np.float32)).astype(jnp.bfloat16)])

    def members(count):
        size = block // count
        return [np.concatenate([index[p * size : (p + 1) * size] + block * i for i in (0, 1)]) for p in range(count)]

    forward = np.stack([both[:, :, m] for m in members(IN_PARTS)])
    backward = np.stack([both[:, m, :] for m in members(parts)])
    turn = 2.0 * np.pi * np.outer(index, np.arange(blocks) + 0.5) / (2 * blocks * block)
    twiddle = np.zeros((block, LANES), np.float32)
    twiddle[:, :blocks] = np.cos(turn)
    twiddle[:, blocks : 2 * blocks] = np.sin(turn)
    return forward, backward, twiddle


def weighted(terms):
    total = None
    for weight, term in terms:
        part = term if weight == 1.0 else term * np.float32(weight)
        total = part if total is None else total + part
    return total


def kernel(
    blocks, chans, parts,
    values_hbm, gates_hbm, filters_hbm, skip, forward_hbm, backward_hbm, twiddle, w_hbm,
    out,
    values, gates, filters, h_send, got_v, got_h, forward, backward, z, spec_v, spec_h, y, d, y_send, causal, mixed, w, acc,
    l_sem, v_out, v_in, h_out, h_in, c_out, c_in, a_out, a_in, b_out, b_in, f_out, f_in,
):
    me = lax.axis_index("seq")
    mine = lax.axis_index("chan")
    block = values.shape[0]
    half = blocks // 2
    piece = block // IN_PARTS
    chunk = block // parts

    def columns(position):
        return pl.ds(pl.multiple_of(position * LANES, LANES), LANES)

    def ahead(step):
        return lax.rem(me + step, blocks)

    def behind(step):
        return lax.rem(me + blocks - step, blocks)

    local = [
        pltpu.make_async_copy(source, target, l_sem.at[i])
        for i, (source, target) in enumerate((
            (filters_hbm, filters), (values_hbm, values), (values_hbm.at[:, columns(me)], got_v.at[me]),
            (forward_hbm, forward), (backward_hbm, backward), (gates_hbm, gates), (w_hbm, w),
        ))
    ]
    filters_copy, values_copy, own_copy, forward_copy, backward_copy, gates_copy, w_copy = local
    for copy in local:
        copy.start()

    sibling = mine + 1 - 2 * lax.rem(mine, 2)
    across = lax.rem(mine + 2, chans)
    barrier = pltpu.get_barrier_semaphore()
    for step in range(1, blocks):
        pl.semaphore_signal(barrier, inc=1, device_id={"seq": ahead(step)}, device_id_type=MESH)
    for other in (sibling, across):
        pl.semaphore_signal(barrier, inc=1, device_id={"chan": other}, device_id_type=MESH)
    pl.semaphore_wait(barrier, blocks + 1)

    def exchange(source, target, out_sem, in_sem, part, step):
        rows = pl.ds(part * piece, piece)
        return pltpu.make_async_remote_copy(
            src_ref=source.at[rows, columns(ahead(step))],
            dst_ref=target.at[me, rows],
            send_sem=out_sem.at[part, step],
            recv_sem=in_sem.at[part, step],
            device_id={"seq": ahead(step)},
            device_id_type=MESH,
        )

    order = sorted(range(1, blocks), key=lambda step: -min(step, blocks - step))
    v_copies = [[exchange(values_hbm, got_v, v_out, v_in, part, step) for step in order] for part in range(IN_PARTS)]
    for copies in v_copies:
        for copy in copies:
            copy.start()
    filters_copy.wait()
    h_copies = [[exchange(h_send, got_h, h_out, h_in, part, step) for step in order] for part in range(IN_PARTS)]
    for part in range(IN_PARTS):
        rows = pl.ds(part * piece, piece)
        h_send[rows, :] = filters[rows, :].astype(jnp.bfloat16)
        for copy in h_copies[part]:
            copy.start()
    got_h[me] = h_send[:, columns(me)]
    own_copy.wait()
    forward_copy.wait()

    def spread(got, part):
        def body(strip, _):
            here = pl.multiple_of(strip * STRIP, STRIP)
            rows = pl.ds(part * piece + here, STRIP)
            x = [got[n, rows, :].astype(jnp.float32) for n in range(blocks)]
            for r in range(half):
                phi = math.pi * (2 * r + 1) / (2 * blocks)
                sums = []
                for odd in (0, 1):
                    picks = range(odd, blocks, 2)
                    sums.append(weighted([(math.cos(phi * n), x[n]) for n in picks]))
                    sums.append(weighted([(-math.sin(phi * n), x[n]) for n in picks if n]))
                even_re, even_im, odd_re, odd_im = sums
                for res, re, im in (
                    (r, even_re + odd_re, even_im + odd_im),
                    (blocks - 1 - r, even_re - odd_re, odd_im - even_im),
                ):
                    cos = twiddle[rows, res : res + 1]
                    sin = twiddle[rows, blocks + res : blocks + res + 1]
                    lanes = slice(res % 2 * LANES, (res % 2 + 1) * LANES)
                    re_high, re_low = split(re * cos + im * sin)
                    im_high, im_low = split(im * cos - re * sin)
                    for place, value in enumerate((re_high, im_high, re_low, im_low)):
                        z[res // 2, pl.ds(place * piece + here, STRIP), lanes] = value
            return 0

        lax.fori_loop(0, piece // STRIP, body, 0)

    def times(high, low, x):
        middle = x.shape[0] // 2
        return (
            jnp.dot(high, x[:middle], preferred_element_type=jnp.float32)
            + jnp.dot(low, x[:middle], preferred_element_type=jnp.float32)
            + jnp.dot(high, x[middle:], preferred_element_type=jnp.float32)
        )

    def transform(spectrum, part):
        def body(pair, _):
            x = times(forward[part, 0], forward[part, 1], z[pair])
            spectrum[pair] = spectrum[pair] + x if part else x
            return 0

        lax.fori_loop(0, half, body, 0)

    for got, copies, spectrum in ((got_v, v_copies, spec_v), (got_h, h_copies, spec_h)):
        for part in range(IN_PARTS):
            for copy in copies[part]:
                copy.wait_recv()
            spread(got, part)
            transform(spectrum, part)

    def product(pair, _):
        re_v, re_h = spec_v[pair, :block], spec_h[pair, :block]
        im_v, im_h = spec_v[pair, block:], spec_h[pair, block:]
        re_high, re_low = split(re_v * re_h - im_v * im_h)
        im_high, im_low = split(-(re_v * im_h + im_v * re_h))
        for place, value in enumerate((re_high, im_high, re_low, im_low)):
            y[pair, place * block : (place + 1) * block] = value
        return 0

    lax.fori_loop(0, half, product, 0)
    backward_copy.wait()

    def undo(part):
        def inverse(pair, _):
            d[pair] = times(backward[part, 0], backward[part, 1], y[pair])
            return 0

        lax.fori_loop(0, half, inverse, 0)

        def body(strip, _):
            here = pl.multiple_of(strip * STRIP, STRIP)
            rows = pl.ds(part * chunk + here, STRIP)
            scale = 1.0 / (blocks * block)
            sums = []
            for r in range(half):
                turned = []
                for res in (r, blocks - 1 - r):
                    lanes = slice(res % 2 * LANES, (res % 2 + 1) * LANES)
                    re = d[res // 2, pl.ds(here, STRIP), lanes]
                    im = -d[res // 2, pl.ds(chunk + here, STRIP), lanes]
                    cos = twiddle[rows, res : res + 1]
                    sin = twiddle[rows, blocks + res : blocks + res + 1]
                    turned.append((re * cos - im * sin, im * cos + re * sin))
                (re_a, im_a), (re_b, im_b) = turned
                sums.append(((re_a + re_b, im_a - im_b), (re_a - re_b, im_a + im_b)))
            for n in range(blocks):
                terms = []
                for r in range(half):
                    phi = math.pi * (2 * r + 1) / (2 * blocks)
                    re, im = sums[r][n % 2]
                    terms.append((scale * math.cos(phi * n), re))
                    if n:
                        terms.append((-scale * math.sin(phi * n), im))
                y_send[n, rows, :] = weighted(terms).astype(jnp.bfloat16)
            return 0

        lax.fori_loop(0, chunk // STRIP, body, 0)

    def back(part, step):
        rows = pl.ds(part * chunk, chunk)
        return pltpu.make_async_remote_copy(
            src_ref=y_send.at[ahead(step), rows],
            dst_ref=causal.at[me, rows],
            send_sem=c_out.at[part, step],
            recv_sem=c_in.at[part, step],
            device_id={"seq": ahead(step)},
            device_id_type=MESH,
        )

    c_copies = [[back(part, step) for step in order] for part in range(parts)]

    def send(part):
        for copy in c_copies[part]:
            copy.start()
        rows = pl.ds(part * chunk, chunk)
        causal[me, rows] = y_send[me, rows]

    def share(source_chan, target, out_sem, in_sem, part):
        spot = mixed.at[source_chan, pl.ds(part * chunk, chunk)]
        return pltpu.make_async_remote_copy(
            src_ref=spot, dst_ref=spot,
            send_sem=out_sem.at[part], recv_sem=in_sem.at[part],
            device_id={"chan": target}, device_id_type=MESH,
        )

    depth = values.shape[1]
    a_copies = [share(mine, across, a_out, a_in, part) for part in range(parts)]
    b_copies = [share(mine, sibling, b_out, b_in, part) for part in range(parts)]
    f_copies = [share(across, sibling, f_out, f_in, part) for part in range(parts)]
    opposite = lax.rem(sibling + 2, chans)

    def blend(part):
        rows = pl.ds(part * chunk, chunk)
        for source in range(blocks):
            cols = slice(source * LANES, (source + 1) * LANES)
            direct = skip[:, cols] * values[rows, cols].astype(jnp.float32)
            mixed[mine, rows, cols] = (
                gates[rows, cols].astype(jnp.float32) * (causal[source, rows].astype(jnp.float32) + direct)
            ).astype(jnp.bfloat16)

    def project(part, pair, last):
        rows = pl.ds(part * chunk, chunk)

        def tile(n, _):
            cols = pl.ds(pl.multiple_of(n * 256, 256), 256)
            total = None
            for which in pair:
                deep = pl.ds(pl.multiple_of(which * depth, depth), depth)
                term = jnp.dot(mixed[which, rows], w[deep, cols], preferred_element_type=jnp.float32)
                total = term if total is None else total + term
            if last:
                out[rows, cols] = (total + acc[rows, cols]).astype(out.dtype)
            else:
                acc[rows, cols] = total
            return 0

        lax.fori_loop(0, out.shape[1] // 256, tile, 0)

    def receive(part):
        for copy in c_copies[part]:
            copy.wait_recv()
        blend(part)
        a_copies[part].start()
        b_copies[part].start()

    def forward_on(part):
        a_copies[part].wait_recv()
        f_copies[part].start()

    def near(part):
        b_copies[part].wait_recv()
        project(part, (mine, sibling), False)

    def far(part):
        f_copies[part].wait_recv()
        project(part, (across, opposite), True)

    values_copy.wait()
    gates_copy.wait()
    lag = min(LAG, parts)
    for part in range(parts):
        undo(part)
        if part >= lag:
            receive(part - lag)
            if part > lag:
                forward_on(part - lag - 1)
        send(part)
    w_copy.wait()
    for part in range(parts - lag):
        near(part)
    for part in range(parts - lag, parts):
        receive(part)
        if part >= 1:
            forward_on(part - 1)
        if part >= 2:
            far(part - 2)
        near(part)
    forward_on(parts - 1)
    if parts >= 2:
        far(parts - 2)
    far(parts - 1)
    for copies in v_copies + h_copies + c_copies + [a_copies, b_copies, f_copies]:
        for copy in copies:
            copy.wait_send()


def per_device_fused(blocks, chans, values, gates, filters, skip, w_out):
    block, width = values.shape
    parts = OUT_PARTS
    forward, backward, twiddle = tables(blocks, block, parts)
    vmem = pl.BlockSpec(memory_space=pltpu.VMEM)
    hbm = pl.BlockSpec(memory_space=pl.ANY)
    half = blocks // 2
    out_width = w_out.shape[1]

    def sems(*shape):
        return pltpu.SemaphoreType.DMA(shape)

    return pl.pallas_call(
        functools.partial(kernel, blocks, chans, parts),
        out_shape=jax.ShapeDtypeStruct((block, out_width), jnp.bfloat16),
        in_specs=[hbm, hbm, hbm, vmem, hbm, hbm, vmem, hbm],
        out_specs=vmem,
        scratch_shapes=[
            pltpu.VMEM((block, width), jnp.bfloat16),
            pltpu.VMEM((block, width), jnp.bfloat16),
            pltpu.VMEM((block, width), jnp.float32),
            pltpu.VMEM((block, width), jnp.bfloat16),
            pltpu.VMEM((blocks, block, LANES), jnp.bfloat16),
            pltpu.VMEM((blocks, block, LANES), jnp.bfloat16),
            pltpu.VMEM(forward.shape, jnp.bfloat16),
            pltpu.VMEM(backward.shape, jnp.bfloat16),
            pltpu.VMEM((half, 4 * block // IN_PARTS, 2 * LANES), jnp.bfloat16),
            pltpu.VMEM((half, 2 * block, 2 * LANES), jnp.float32),
            pltpu.VMEM((half, 2 * block, 2 * LANES), jnp.float32),
            pltpu.VMEM((half, 4 * block, 2 * LANES), jnp.bfloat16),
            pltpu.VMEM((half, 2 * block // parts, 2 * LANES), jnp.float32),
            pltpu.VMEM((blocks, block, LANES), jnp.bfloat16),
            pltpu.VMEM((blocks, block, LANES), jnp.bfloat16),
            pltpu.VMEM((chans, block, width), jnp.bfloat16),
            pltpu.VMEM(w_out.shape, jnp.bfloat16),
            pltpu.VMEM((block, out_width), jnp.float32),
            sems(7),
        ]
        + [sems(IN_PARTS, blocks)] * 4
        + [sems(parts, blocks)] * 2
        + [sems(parts)] * 6,
        compiler_params=pltpu.CompilerParams(
            collective_id=0, has_side_effects=True, vmem_limit_bytes=56 * 2**20
        ),
    )(values, gates, filters, skip[None, :], jnp.asarray(forward), jnp.asarray(backward), jnp.asarray(twiddle), w_out)


def per_device(mesh_shape, values, gates, filters, skip, w_out):
    blocks, chans = mesh_shape["seq"], mesh_shape["chan"]
    block, width = values.shape
    fits = (
        width == blocks * LANES and chans == 4 and blocks % 2 == 0 and blocks <= 16
        and block % 256 == 0 and block <= 512 and w_out.shape[1] % 256 == 0
    )
    if fits:
        return per_device_fused(blocks, chans, values, gates, filters, skip, w_out)
    return per_device_generic(values, gates, filters, skip, w_out)


def solution(mesh):
    placed = (P("seq", "chan"), P("seq", "chan"), P("seq", "chan"), P("chan"), P(None, "chan"))
    return jax.shard_map(
        functools.partial(per_device, dict(mesh.shape)),
        mesh=mesh, in_specs=placed, out_specs=P("seq", "chan"), check_vma=False,
    )
```

```python
import functools
import math

import jax
import jax.numpy as jnp
import numpy as np
from jax import lax
from jax.experimental import pallas as pl
from jax.experimental.pallas import tpu as pltpu
from jax.sharding import PartitionSpec as P

LANES = 128
STRIP = 16
IN_PARTS = 2
OUT_PARTS = 4
MESH = pl.DeviceIdType.MESH


def product(form, left, right):
    return jnp.einsum(
        form, left, right, precision=lax.Precision.HIGHEST, preferred_element_type=jnp.float32
    )


def phase(first_count, second_count, modulus):
    left = lax.iota(jnp.int32, first_count)[:, None]
    right = lax.iota(jnp.int32, second_count)[None, :]
    angle = (left * right % modulus).astype(jnp.float32) * (2.0 * math.pi / modulus)
    return (jnp.cos(angle), jnp.sin(angle))


def spectral_conv(chan_values, chan_filter):
    nchan = chan_values.shape[0]
    length = chan_values.shape[1]
    summed = 2 * length
    columns = 128
    row_count = summed // columns
    half_rows = row_count // 2
    cos_rows, sin_rows = phase(row_count, half_rows, row_count)
    cos_twist, sin_twist = phase(row_count, columns, summed)
    cos_cols, sin_cols = phase(columns, columns, columns)
    cos_back, sin_back = phase(half_rows, row_count, row_count)

    def forward(signal):
        grid = signal.astype(jnp.float32).reshape(nchan, half_rows, columns)
        real_a = product("kn,cna->cka", cos_rows, grid)
        imag_a = -product("kn,cna->cka", sin_rows, grid)
        real_b = real_a * cos_twist + imag_a * sin_twist
        imag_b = imag_a * cos_twist - real_a * sin_twist
        real_c = product("cka,am->ckm", real_b, cos_cols) + product("cka,am->ckm", imag_b, sin_cols)
        imag_c = product("cka,am->ckm", imag_b, cos_cols) - product("cka,am->ckm", real_b, sin_cols)
        return (real_c, imag_c)

    real_v, imag_v = forward(chan_values)
    real_h, imag_h = forward(chan_filter)
    real_p = real_v * real_h - imag_v * imag_h
    imag_p = real_v * imag_h + imag_v * real_h
    real_d = product("ckm,ma->cka", real_p, cos_cols) - product("ckm,ma->cka", imag_p, sin_cols)
    imag_d = product("ckm,ma->cka", imag_p, cos_cols) + product("ckm,ma->cka", real_p, sin_cols)
    real_e = real_d * cos_twist - imag_d * sin_twist
    imag_e = imag_d * cos_twist + real_d * sin_twist
    result = product("nk,cka->cna", cos_back, real_e) - product("nk,cka->cna", sin_back, imag_e)
    return (result * (1.0 / summed)).reshape(nchan, length).astype(jnp.bfloat16)


def per_device_generic(values, gates, filters, skip, w_out):
    value_trans = values.T
    filter_trans = filters.T
    chan_values = lax.all_to_all(value_trans, "seq", split_axis=0, concat_axis=1, tiled=True)
    chan_filter = lax.all_to_all(filter_trans, "seq", split_axis=0, concat_axis=1, tiled=True)
    convolved = spectral_conv(chan_values, chan_filter)
    causal_trans = lax.all_to_all(convolved, "seq", split_axis=1, concat_axis=0, tiled=True)
    causal = causal_trans.T
    mixed = (
        gates.astype(jnp.float32)
        * (causal.astype(jnp.float32) + skip[None, :] * values.astype(jnp.float32))
    ).astype(jnp.bfloat16)
    projected = jnp.dot(
        lax.all_gather(mixed, "chan", axis=1, tiled=True), w_out, preferred_element_type=jnp.float32
    )
    return projected.astype(jnp.bfloat16)


def split(x):
    high = x.astype(jnp.bfloat16)
    return high, (x - high.astype(jnp.float32)).astype(jnp.bfloat16)


def tables(blocks, block, parts):
    index = np.arange(block)
    angle = 2.0 * np.pi * (np.outer(index, index) % block) / block
    cos, sin = np.cos(angle), np.sin(angle)
    whole = np.block([[cos, sin], [-sin, cos]]).astype(np.float32)
    high = whole.astype(jnp.bfloat16)
    both = np.stack([high, (whole - high.astype(np.float32)).astype(jnp.bfloat16)])

    def members(count):
        size = block // count
        return [np.concatenate([index[p * size : (p + 1) * size] + block * i for i in (0, 1)]) for p in range(count)]

    forward = np.stack([both[:, :, m] for m in members(IN_PARTS)])
    backward = np.stack([both[:, m, :] for m in members(parts)])
    turn = 2.0 * np.pi * np.outer(index, np.arange(blocks) + 0.5) / (2 * blocks * block)
    twiddle = np.zeros((block, LANES), np.float32)
    twiddle[:, :blocks] = np.cos(turn)
    twiddle[:, blocks : 2 * blocks] = np.sin(turn)
    return forward, backward, twiddle


def weighted(terms):
    total = None
    for weight, term in terms:
        part = term if weight == 1.0 else term * np.float32(weight)
        total = part if total is None else total + part
    return total


def kernel(
    blocks, chans, parts,
    values_hbm, gates_hbm, filters_hbm, skip, forward_hbm, backward_hbm, twiddle, w_hbm,
    out,
    values, gates, filters, h_send, got_v, got_h, forward, backward, z, spec_v, spec_h, y, d, y_send, causal, mixed, w, acc,
    l_sem, v_out, v_in, h_out, h_in, c_out, c_in, a_out, a_in, b_out, b_in, f_out, f_in,
):
    me = lax.axis_index("seq")
    mine = lax.axis_index("chan")
    block = values.shape[0]
    half = blocks // 2
    piece = block // IN_PARTS
    chunk = block // parts

    def columns(position):
        return pl.ds(pl.multiple_of(position * LANES, LANES), LANES)

    def ahead(step):
        return lax.rem(me + step, blocks)

    def behind(step):
        return lax.rem(me + blocks - step, blocks)

    local = [
        pltpu.make_async_copy(source, target, l_sem.at[i])
        for i, (source, target) in enumerate((
            (filters_hbm, filters), (values_hbm, values), (values_hbm.at[:, columns(me)], got_v.at[me]),
            (forward_hbm, forward), (backward_hbm, backward), (gates_hbm, gates), (w_hbm, w),
        ))
    ]
    filters_copy, values_copy, own_copy, forward_copy, backward_copy, gates_copy, w_copy = local
    for copy in local:
        copy.start()

    sibling = mine + 1 - 2 * lax.rem(mine, 2)
    across = lax.rem(mine + 2, chans)
    barrier = pltpu.get_barrier_semaphore()
    for step in range(1, blocks):
        pl.semaphore_signal(barrier, inc=1, device_id={"seq": ahead(step)}, device_id_type=MESH)
    for other in (sibling, across):
        pl.semaphore_signal(barrier, inc=1, device_id={"chan": other}, device_id_type=MESH)
    pl.semaphore_wait(barrier, blocks + 1)

    def exchange(source, target, out_sem, in_sem, part, step):
        rows = pl.ds(part * piece, piece)
        return pltpu.make_async_remote_copy(
            src_ref=source.at[rows, columns(ahead(step))],
            dst_ref=target.at[me, rows],
            send_sem=out_sem.at[part, step],
            recv_sem=in_sem.at[part, step],
            device_id={"seq": ahead(step)},
            device_id_type=MESH,
        )

    order = sorted(range(1, blocks), key=lambda step: -min(step, blocks - step))
    v_copies = [[exchange(values_hbm, got_v, v_out, v_in, part, step) for step in order] for part in range(IN_PARTS)]
    for copies in v_copies:
        for copy in copies:
            copy.start()
    filters_copy.wait()
    h_copies = [[exchange(h_send, got_h, h_out, h_in, part, step) for step in order] for part in range(IN_PARTS)]
    for part in range(IN_PARTS):
        rows = pl.ds(part * piece, piece)
        h_send[rows, :] = filters[rows, :].astype(jnp.bfloat16)
        for copy in h_copies[part]:
            copy.start()
    got_h[me] = h_send[:, columns(me)]
    own_copy.wait()
    forward_copy.wait()

    def spread(got, part):
        def body(strip, _):
            here = pl.multiple_of(strip * STRIP, STRIP)
            rows = pl.ds(part * piece + here, STRIP)
            x = [got[n, rows, :].astype(jnp.float32) for n in range(blocks)]
            for r in range(half):
                phi = math.pi * (2 * r + 1) / (2 * blocks)
                sums = []
                for odd in (0, 1):
                    picks = range(odd, blocks, 2)
                    sums.append(weighted([(math.cos(phi * n), x[n]) for n in picks]))
                    sums.append(weighted([(-math.sin(phi * n), x[n]) for n in picks if n]))
                even_re, even_im, odd_re, odd_im = sums
                for res, re, im in (
                    (r, even_re + odd_re, even_im + odd_im),
                    (blocks - 1 - r, even_re - odd_re, odd_im - even_im),
                ):
                    cos = twiddle[rows, res : res + 1]
                    sin = twiddle[rows, blocks + res : blocks + res + 1]
                    lanes = slice(res % 2 * LANES, (res % 2 + 1) * LANES)
                    re_high, re_low = split(re * cos + im * sin)
                    im_high, im_low = split(im * cos - re * sin)
                    for place, value in enumerate((re_high, im_high, re_low, im_low)):
                        z[res // 2, pl.ds(place * piece + here, STRIP), lanes] = value
            return 0

        lax.fori_loop(0, piece // STRIP, body, 0)

    def times(high, low, x):
        middle = x.shape[0] // 2
        return (
            jnp.dot(high, x[:middle], preferred_element_type=jnp.float32)
            + jnp.dot(low, x[:middle], preferred_element_type=jnp.float32)
            + jnp.dot(high, x[middle:], preferred_element_type=jnp.float32)
        )

    def transform(spectrum, part):
        def body(pair, _):
            x = times(forward[part, 0], forward[part, 1], z[pair])
            spectrum[pair] = spectrum[pair] + x if part else x
            return 0

        lax.fori_loop(0, half, body, 0)

    for got, copies, spectrum in ((got_v, v_copies, spec_v), (got_h, h_copies, spec_h)):
        for part in range(IN_PARTS):
            for copy in copies[part]:
                copy.wait_recv()
            spread(got, part)
            transform(spectrum, part)

    def product(pair, _):
        re_v, re_h = spec_v[pair, :block], spec_h[pair, :block]
        im_v, im_h = spec_v[pair, block:], spec_h[pair, block:]
        re_high, re_low = split(re_v * re_h - im_v * im_h)
        im_high, im_low = split(-(re_v * im_h + im_v * re_h))
        for place, value in enumerate((re_high, im_high, re_low, im_low)):
            y[pair, place * block : (place + 1) * block] = value
        return 0

    lax.fori_loop(0, half, product, 0)
    backward_copy.wait()

    def undo(part):
        def inverse(pair, _):
            d[pair] = times(backward[part, 0], backward[part, 1], y[pair])
            return 0

        lax.fori_loop(0, half, inverse, 0)

        def body(strip, _):
            here = pl.multiple_of(strip * STRIP, STRIP)
            rows = pl.ds(part * chunk + here, STRIP)
            scale = 1.0 / (blocks * block)
            sums = []
            for r in range(half):
                turned = []
                for res in (r, blocks - 1 - r):
                    lanes = slice(res % 2 * LANES, (res % 2 + 1) * LANES)
                    re = d[res // 2, pl.ds(here, STRIP), lanes]
                    im = -d[res // 2, pl.ds(chunk + here, STRIP), lanes]
                    cos = twiddle[rows, res : res + 1]
                    sin = twiddle[rows, blocks + res : blocks + res + 1]
                    turned.append((re * cos - im * sin, im * cos + re * sin))
                (re_a, im_a), (re_b, im_b) = turned
                sums.append(((re_a + re_b, im_a - im_b), (re_a - re_b, im_a + im_b)))
            for n in range(blocks):
                terms = []
                for r in range(half):
                    phi = math.pi * (2 * r + 1) / (2 * blocks)
                    re, im = sums[r][n % 2]
                    terms.append((scale * math.cos(phi * n), re))
                    if n:
                        terms.append((-scale * math.sin(phi * n), im))
                y_send[n, rows, :] = weighted(terms).astype(jnp.bfloat16)
            return 0

        lax.fori_loop(0, chunk // STRIP, body, 0)

    def back(part, step):
        rows = pl.ds(part * chunk, chunk)
        return pltpu.make_async_remote_copy(
            src_ref=y_send.at[ahead(step), rows],
            dst_ref=causal.at[me, rows],
            send_sem=c_out.at[part, step],
            recv_sem=c_in.at[part, step],
            device_id={"seq": ahead(step)},
            device_id_type=MESH,
        )

    c_copies = [[back(part, step) for step in order] for part in range(parts)]

    def send(part):
        for copy in c_copies[part]:
            copy.start()
        rows = pl.ds(part * chunk, chunk)
        causal[me, rows] = y_send[me, rows]

    def share(source_chan, target, out_sem, in_sem, part):
        spot = mixed.at[source_chan, pl.ds(part * chunk, chunk)]
        return pltpu.make_async_remote_copy(
            src_ref=spot, dst_ref=spot,
            send_sem=out_sem.at[part], recv_sem=in_sem.at[part],
            device_id={"chan": target}, device_id_type=MESH,
        )

    depth = values.shape[1]
    a_copies = [share(mine, across, a_out, a_in, part) for part in range(parts)]
    b_copies = [share(mine, sibling, b_out, b_in, part) for part in range(parts)]
    f_copies = [share(across, sibling, f_out, f_in, part) for part in range(parts)]
    opposite = lax.rem(sibling + 2, chans)

    def blend(part):
        rows = pl.ds(part * chunk, chunk)
        for source in range(blocks):
            cols = slice(source * LANES, (source + 1) * LANES)
            direct = skip[:, cols] * values[rows, cols].astype(jnp.float32)
            mixed[mine, rows, cols] = (
                gates[rows, cols].astype(jnp.float32) * (causal[source, rows].astype(jnp.float32) + direct)
            ).astype(jnp.bfloat16)

    def project(group, pair, last):
        rows = pl.ds(group * 2 * chunk, 2 * chunk)

        def tile(n, _):
            cols = pl.ds(pl.multiple_of(n * 512, 512), 512)
            total = None
            for which in pair:
                deep = pl.ds(pl.multiple_of(which * depth, depth), depth)
                term = jnp.dot(mixed[which, rows], w[deep, cols], preferred_element_type=jnp.float32)
                total = term if total is None else total + term
            if last:
                out[rows, cols] = (total + acc[rows, cols]).astype(out.dtype)
            else:
                acc[rows, cols] = total
            return 0

        lax.fori_loop(0, out.shape[1] // 512, tile, 0)

    def receive(part):
        for copy in c_copies[part]:
            copy.wait_recv()
        blend(part)
        a_copies[part].start()
        b_copies[part].start()

    def forward_on(part):
        a_copies[part].wait_recv()
        f_copies[part].start()

    def near(group):
        for part in (2 * group, 2 * group + 1):
            b_copies[part].wait_recv()
        project(group, (mine, sibling), False)

    def far(group):
        for part in (2 * group, 2 * group + 1):
            f_copies[part].wait_recv()
        project(group, (across, opposite), True)

    values_copy.wait()
    gates_copy.wait()
    undo(0)
    send(0)
    undo(1)
    send(1)
    undo(2)
    receive(0)
    send(2)
    undo(3)
    receive(1)
    forward_on(0)
    send(3)
    w_copy.wait()
    near(0)
    receive(2)
    forward_on(1)
    far(0)
    receive(3)
    forward_on(2)
    near(1)
    forward_on(3)
    far(1)
    for copies in v_copies + h_copies + c_copies + [a_copies, b_copies, f_copies]:
        for copy in copies:
            copy.wait_send()


def per_device_fused(blocks, chans, values, gates, filters, skip, w_out):
    block, width = values.shape
    parts = OUT_PARTS
    forward, backward, twiddle = tables(blocks, block, parts)
    vmem = pl.BlockSpec(memory_space=pltpu.VMEM)
    hbm = pl.BlockSpec(memory_space=pl.ANY)
    half = blocks // 2
    out_width = w_out.shape[1]

    def sems(*shape):
        return pltpu.SemaphoreType.DMA(shape)

    return pl.pallas_call(
        functools.partial(kernel, blocks, chans, parts),
        out_shape=jax.ShapeDtypeStruct((block, out_width), jnp.bfloat16),
        in_specs=[hbm, hbm, hbm, vmem, hbm, hbm, vmem, hbm],
        out_specs=vmem,
        scratch_shapes=[
            pltpu.VMEM((block, width), jnp.bfloat16),
            pltpu.VMEM((block, width), jnp.bfloat16),
            pltpu.VMEM((block, width), jnp.float32),
            pltpu.VMEM((block, width), jnp.bfloat16),
            pltpu.VMEM((blocks, block, LANES), jnp.bfloat16),
            pltpu.VMEM((blocks, block, LANES), jnp.bfloat16),
            pltpu.VMEM(forward.shape, jnp.bfloat16),
            pltpu.VMEM(backward.shape, jnp.bfloat16),
            pltpu.VMEM((half, 4 * block // IN_PARTS, 2 * LANES), jnp.bfloat16),
            pltpu.VMEM((half, 2 * block, 2 * LANES), jnp.float32),
            pltpu.VMEM((half, 2 * block, 2 * LANES), jnp.float32),
            pltpu.VMEM((half, 4 * block, 2 * LANES), jnp.bfloat16),
            pltpu.VMEM((half, 2 * block // parts, 2 * LANES), jnp.float32),
            pltpu.VMEM((blocks, block, LANES), jnp.bfloat16),
            pltpu.VMEM((blocks, block, LANES), jnp.bfloat16),
            pltpu.VMEM((chans, block, width), jnp.bfloat16),
            pltpu.VMEM(w_out.shape, jnp.bfloat16),
            pltpu.VMEM((block, out_width), jnp.float32),
            sems(7),
        ]
        + [sems(IN_PARTS, blocks)] * 4
        + [sems(parts, blocks)] * 2
        + [sems(parts)] * 6,
        compiler_params=pltpu.CompilerParams(
            collective_id=0, has_side_effects=True, vmem_limit_bytes=56 * 2**20
        ),
    )(values, gates, filters, skip[None, :], jnp.asarray(forward), jnp.asarray(backward), jnp.asarray(twiddle), w_out)


def per_device(mesh_shape, values, gates, filters, skip, w_out):
    blocks, chans = mesh_shape["seq"], mesh_shape["chan"]
    block, width = values.shape
    fits = (
        width == blocks * LANES and chans == 4 and blocks % 2 == 0 and blocks <= 16
        and block % 256 == 0 and block <= 512 and w_out.shape[1] % 512 == 0
    )
    if fits:
        return per_device_fused(blocks, chans, values, gates, filters, skip, w_out)
    return per_device_generic(values, gates, filters, skip, w_out)


def solution(mesh):
    placed = (P("seq", "chan"), P("seq", "chan"), P("seq", "chan"), P("chan"), P(None, "chan"))
    return jax.shard_map(
        functools.partial(per_device, dict(mesh.shape)),
        mesh=mesh, in_specs=placed, out_specs=P("seq", "chan"), check_vma=False,
    )
```
